32 devices in a mesh: dp: 4 (over y, core), expert: 2 (over x), tensor: 4 (over z).
Axes of the slice: x: 2, y: 2, z: 4, core: 2. Of those that a mesh axis runs over, the one named last changes fastest.
Arguments:
- inputs: bfloat16 [1576, 768], P(('dp', 'expert')), may hold values from -6 to 6
- first_gain: float32 [768], replicated, may hold values from 0.5 to 1.5
- first_bias: float32 [768], replicated, may hold values from -2 to 2
- attention_in: bfloat16 [3, 768, 768], P(None, None, 'tensor')
- attention_out: bfloat16 [768, 768], P('tensor'), may hold values from -0.875 to 0.875
- second_gain: float32 [768], replicated, may hold values from 0.5 to 1.5
- second_bias: float32 [768], replicated, may hold values from -2 to 2
- router_weight: float32 [768, 4], replicated
- expert_in: bfloat16 [4, 768, 3072], P('expert', None, 'tensor'), may hold values from -0.21875 to 0.21875
- expert_out: bfloat16 [4, 3072, 768], P('expert', 'tensor'), may hold values from -1.75 to 1.75
- expert_ids: int32 [1576, 2], P(('dp', 'expert')), may hold values from 0 to 3, as said below
- slot_index: int32 [1576, 2], P(('dp', 'expert')), may hold values from 0 to 98, as said below
- cotangent: bfloat16 [1576, 768], P(('dp', 'expert')), may hold values from -6 to 6
Outputs:
- layer_out: float32 [1576, 768], P(('dp', 'expert'))
- input_grad: float32 [1576, 768], P(('dp', 'expert'))
- first_gain_grad: float32 [768], P(('dp', 'expert'))
- first_bias_grad: float32 [768], P(('dp', 'expert'))
- attention_in_grad: float32 [3, 768, 768], P(None, ('dp', 'expert'), 'tensor')
- attention_out_grad: float32 [768, 768], P('tensor', ('dp', 'expert'))
- second_gain_grad: float32 [768], P(('dp', 'expert'))
- second_bias_grad: float32 [768], P(('dp', 'expert'))
- router_grad: float32 [768, 4], P(('dp', 'expert'))
- expert_in_grad: float32 [4, 768, 3072], P('expert', 'dp', 'tensor')
- expert_out_grad: float32 [4, 3072, 768], P('expert', 'tensor', 'dp')
The draws below stay inside these ranges and needn't reach their ends.
Inputs may be any that keep to these rules, and one draw needn't show every extreme that they name: `expert_ids`: the two experts of a token differ. `slot_index`: among the 197 tokens of one index of dp and expert, the choices naming one expert hold slots 0, 1, 2 and so on, all first choices before all second choices, rows in order within each; a choice ranked 98 or later holds 98 and is dropped. Some expert fills all 98 slots from every index of dp and expert.
All inputs are finite; a program needn't handle non-finite values.
Results may differ from the reference program's by a relative error of at most 0.02.
Values may be sent and summed in bfloat16 or wider, within the bound.
A program may use at most 128 MiB of HBM per device.

```python
import math
import jax
import jax.numpy as jnp
from jax import lax

D = 768
HEADS = 12
HEAD_DIM = 64
FF = 3072
SEQ = 197
IMG_DEV = 1
ROWS = 197
TOKENS = 1576
EXPERTS = 4
CAP = 98


def routing_draw(key):
    base = jax.random.fold_in(key, 11)
    key_order, key_heavy, key_first, key_second = jax.random.split(base, 4)
    order = jax.random.permutation(key_order, EXPERTS).astype(jnp.int32)
    heavy = jax.random.randint(key_heavy, (TOKENS,), 0, 4)
    first = jnp.where(heavy == 0, 0, jax.random.randint(key_first, (TOKENS,), 1, EXPERTS))
    second = (first + jax.random.randint(key_second, (TOKENS,), 1, EXPERTS)) % EXPERTS
    chosen = order[jnp.stack([first, second], axis=1)].astype(jnp.int32)
    blocks = TOKENS // ROWS
    ordered = jnp.concatenate([chosen[:, 0].reshape(blocks, ROWS), chosen[:, 1].reshape(blocks, ROWS)], axis=1)
    onehot = (ordered[:, :, None] == jnp.arange(EXPERTS, dtype=jnp.int32)).astype(jnp.int32)
    ranks = jnp.sum(jnp.cumsum(onehot, axis=1) * onehot, axis=2) - 1
    ranks = jnp.minimum(ranks, CAP)
    slots = jnp.stack([ranks[:, :ROWS].reshape(TOKENS), ranks[:, ROWS:].reshape(TOKENS)], axis=1)
    return (chosen, slots.astype(jnp.int32))


def draw_expert_ids(key, part):
    chosen, slots = routing_draw(key)
    return chosen


def draw_slot_index(key, part):
    chosen, slots = routing_draw(key)
    return slots


def draw_attention_in(key, part):
    width = HEADS * HEAD_DIM
    key_base = jax.random.fold_in(key, 3)
    base = jax.random.normal(key_base, (3, D, width), jnp.float32) / math.sqrt(D)
    return base.astype(jnp.bfloat16)


def draw_router_weight(key, part):
    key_base = jax.random.fold_in(jax.random.fold_in(key, 5), 0)
    return jax.random.normal(key_base, (D, EXPERTS), jnp.float32) * (1.5 / math.sqrt(D))


def block_levels(rng, dims, pieces, least, largest):
    level, own = 1.0, jax.random.fold_in(rng, 6)
    for position, parts in pieces:
        steps = jnp.exp(jax.random.uniform(jax.random.fold_in(own, position), (parts,), jnp.float32, least / len(pieces), largest / len(pieces)))
        level = level * jnp.repeat(steps, dims[position] // parts).reshape([-1 if axis == position else 1 for axis in range(len(dims))])
    return level


def noise(rng, extent, scale, most, pieces=(), kind=jnp.bfloat16):
    level = block_levels(rng, extent, pieces, -0.22, 0.18) if pieces else 1.0
    array = jax.random.normal(rng, extent, jnp.float32) * scale * level
    return jnp.minimum(jnp.maximum(array, -most), most).astype(kind)


def setup_inputs(seed: int = 0) -> dict:
    seeds = jax.random.split(jax.random.key(seed), 14)
    return {
        "inputs": noise(seeds[0], (TOKENS, D), 1.0, 6.0, ((0, 8),)),
        "first_gain": jnp.clip(1.0 + 0.1 * jax.random.normal(seeds[1], (D,), jnp.float32), 0.5, 1.5),
        "first_bias": noise(seeds[2], (D,), 0.3, 2.0, (), jnp.float32),
        "attention_in": draw_attention_in(jax.random.fold_in(seeds[13], 71), 0),
        "attention_out": noise(seeds[4], (HEADS * HEAD_DIM, D), (HEADS * HEAD_DIM // 16) ** -0.5, 0.875, ((0, 4),)),
        "second_gain": jnp.clip(1.0 + 0.1 * jax.random.normal(seeds[5], (D,), jnp.float32), 0.5, 1.5),
        "second_bias": noise(seeds[6], (D,), 0.3, 2.0, (), jnp.float32),
        "router_weight": draw_router_weight(jax.random.fold_in(seeds[13], 71), 0),
        "expert_in": noise(seeds[8], (EXPERTS, D, FF), D ** -0.5, 0.21875, ((0, 2), (2, 4))),
        "expert_out": noise(seeds[9], (EXPERTS, FF, D), (max(1, FF // 256)) ** -0.5, 1.75, ((0, 2), (1, 4))),
        "expert_ids": draw_expert_ids(jax.random.fold_in(seeds[13], 71), 0),
        "slot_index": draw_slot_index(jax.random.fold_in(seeds[13], 71), 0),
        "cotangent": noise(seeds[12], (TOKENS, D), 1.0, 6.0, ((0, 8),)),
    }


EPS = 1e-06
GELU_C = math.sqrt(2.0 / math.pi)

def normalize(values):
    centre = lax.optimization_barrier(jnp.mean(values, axis=-1, keepdims=True))
    centred = values - centre
    spread = lax.optimization_barrier(jnp.mean(centred * centred, axis=-1, keepdims=True))
    scale = lax.rsqrt(spread + EPS)
    return (centred * scale, scale)

def norm_back(grad_out, normed, scale, gain):
    scaled = grad_out * gain
    first_mean = lax.optimization_barrier(jnp.mean(scaled, axis=-1, keepdims=True))
    second_mean = lax.optimization_barrier(jnp.mean(scaled * normed, axis=-1, keepdims=True))
    return scale * (scaled - first_mean - normed * second_mean)

def gelu_parts(pre):
    inner = GELU_C * (pre + 0.044715 * pre * pre * pre)
    tangent = jnp.tanh(inner)
    value = 0.5 * pre * (1.0 + tangent)
    slope = 0.5 * (1.0 + tangent) + 0.5 * pre * (1.0 - tangent * tangent) * GELU_C * (1.0 + 3.0 * 0.044715 * pre * pre)
    return (value, slope)

def reference(inputs, first_gain, first_bias, attention_in, attention_out, second_gain, second_bias, router_weight, expert_in, expert_out, expert_ids, slot_index, cotangent):
    fl = jnp.float32
    bf = jnp.bfloat16
    tokens = inputs.shape[0]
    sources = tokens // ROWS
    width = HEADS * HEAD_DIM
    scaling = HEAD_DIM ** (-0.5)
    x_full = inputs.astype(fl)
    normed1, scale1 = normalize(x_full)
    first = (normed1 * first_gain + first_bias).astype(bf)
    project = [jnp.dot(first, attention_in[which], preferred_element_type=fl).astype(bf) for which in range(3)]

    def blocked(matrix):
        return matrix.reshape(sources, IMG_DEV, SEQ, HEADS, HEAD_DIM)

    def attend(block):
        query, keys, values = [part.astype(fl) for part in block]
        scores = jnp.einsum('iqhd,ikhd->ihqk', query, keys) * scaling
        peak = lax.optimization_barrier(jnp.max(scores, axis=-1, keepdims=True))
        logsum = peak[..., 0] + jnp.log(lax.optimization_barrier(jnp.sum(jnp.exp(scores - peak), axis=-1)))
        probs = jnp.exp(scores - logsum[..., None])
        weights = probs.astype(bf).astype(fl)
        context = jnp.einsum('ihqk,ikhd->iqhd', weights, values).astype(bf)
        return (context, logsum)
    context_b, logsums = lax.map(attend, (blocked(project[0]), blocked(project[1]), blocked(project[2])))
    context = context_b.reshape(tokens, width)
    attended = jnp.dot(context, attention_out, preferred_element_type=fl)
    resid = x_full + attended
    normed2, scale2 = normalize(resid)
    second = (normed2 * second_gain + second_bias).astype(bf)
    logits = jnp.dot(second.astype(fl), router_weight, precision=lax.Precision.HIGHEST)
    route = jax.nn.softmax(logits, axis=-1)
    valid = (slot_index < CAP).astype(fl)
    gate = jnp.take_along_axis(route, expert_ids, axis=1) * valid
    source = jnp.broadcast_to((jnp.arange(tokens, dtype=jnp.int32) // ROWS)[:, None], (tokens, 2))

    def to_slots(rows_both):
        holder = jnp.zeros((EXPERTS, sources, CAP + 1, D), bf)
        holder = holder.at[expert_ids, source, slot_index].set(rows_both)
        return holder[:, :, :CAP].reshape(EXPERTS, sources * CAP, D)

    def from_slots(slotted):
        padded = jnp.concatenate([slotted.reshape(EXPERTS, sources, CAP, D), jnp.zeros((EXPERTS, sources, 1, D), bf)], axis=2)
        return padded[expert_ids, source, slot_index].astype(fl)
    buffer = to_slots(jnp.broadcast_to(second[:, None, :], (tokens, 2, D)))

    def expert_forward(item):
        rows_e, weight_a, weight_b = item
        pre = jnp.dot(rows_e, weight_a, preferred_element_type=fl)
        value, unused = gelu_parts(pre)
        return jnp.dot(value.astype(bf), weight_b, preferred_element_type=fl).astype(bf)
    outputs = lax.map(expert_forward, (buffer, expert_in, expert_out))
    picked = from_slots(outputs)
    layer_out = resid + lax.optimization_barrier(jnp.sum(gate[..., None] * picked, axis=1))
    grad_out = cotangent.astype(fl)
    gate_grad = lax.optimization_barrier(jnp.sum(grad_out[:, None, :] * picked, axis=-1)) * valid
    y_grad = (gate[..., None] * grad_out[:, None, :]).astype(bf)
    grad_buffer = to_slots(y_grad)

    def expert_backward(item):
        rows_e, grads_e, weight_a, weight_b = item
        pre = jnp.dot(rows_e, weight_a, preferred_element_type=fl)
        value, slope = gelu_parts(pre)
        hidden = value.astype(bf)
        hidden_grad = jnp.dot(grads_e, weight_b.T, preferred_element_type=fl)
        pre_grad = (hidden_grad * slope).astype(bf)
        grad_b = jnp.dot(hidden.T, grads_e, preferred_element_type=fl)
        grad_a = jnp.dot(rows_e.T, pre_grad, preferred_element_type=fl)
        back = jnp.dot(pre_grad, weight_a.T, preferred_element_type=fl).astype(bf)
        return (grad_a, grad_b, back)
    expert_in_grad, expert_out_grad, back_buffer = lax.map(expert_backward, (buffer, grad_buffer, expert_in, expert_out))
    back_rows = lax.optimization_barrier(jnp.sum(from_slots(back_buffer), axis=1))
    choose = (expert_ids[:, :, None] == jnp.arange(EXPERTS, dtype=jnp.int32)).astype(fl)
    route_grad = lax.optimization_barrier(jnp.sum(gate_grad[:, :, None] * choose, axis=1))
    logit_grad = route * (route_grad - lax.optimization_barrier(jnp.sum(route * route_grad, axis=-1, keepdims=True)))
    router_grad = jnp.dot(second.astype(fl).T, logit_grad, precision=lax.Precision.HIGHEST)
    second_grad = back_rows + jnp.dot(logit_grad, router_weight.T, precision=lax.Precision.HIGHEST)
    second_gain_grad = lax.optimization_barrier(jnp.sum(second_grad * normed2, axis=0))
    second_bias_grad = lax.optimization_barrier(jnp.sum(second_grad, axis=0))
    resid_grad = grad_out + norm_back(second_grad, normed2, scale2, second_gain)
    resid_low = resid_grad.astype(bf)
    attention_out_grad = jnp.dot(context.T, resid_low, preferred_element_type=fl)
    context_grad = jnp.dot(resid_low, attention_out.T, preferred_element_type=fl).astype(bf)

    def attend_back(block):
        query, keys, values, context_h, context_g, logsum = block
        query, keys, values, context_h, context_g = [part.astype(fl) for part in (query, keys, values, context_h, context_g)]
        scores = jnp.einsum('iqhd,ikhd->ihqk', query, keys) * scaling
        probs = jnp.exp(scores - logsum[..., None])
        weights = probs.astype(bf).astype(fl)
        values_grad = jnp.einsum('ihqk,iqhd->ikhd', weights, context_g).astype(bf)
        probs_grad = jnp.einsum('iqhd,ikhd->ihqk', context_g, values)
        delta = jnp.transpose(lax.optimization_barrier(jnp.sum(context_g * context_h, axis=-1)), (0, 2, 1))
        score_grad = (probs * (probs_grad - delta[..., None]) * scaling).astype(bf).astype(fl)
        query_grad = jnp.einsum('ihqk,ikhd->iqhd', score_grad, keys).astype(bf)
        keys_grad = jnp.einsum('ihqk,iqhd->ikhd', score_grad, query).astype(bf)
        return (query_grad, keys_grad, values_grad)
    grads_qkv = lax.map(attend_back, (blocked(project[0]), blocked(project[1]), blocked(project[2]), context_b, blocked(context_grad), logsums))
    grads_flat = [part.reshape(tokens, width) for part in grads_qkv]
    attention_in_grad = jnp.stack([jnp.dot(first.T, part, preferred_element_type=fl) for part in grads_flat])
    first_grad = jnp.dot(grads_flat[0], attention_in[0].T, preferred_element_type=fl)
    first_grad = first_grad + jnp.dot(grads_flat[1], attention_in[1].T, preferred_element_type=fl)
    first_grad = first_grad + jnp.dot(grads_flat[2], attention_in[2].T, preferred_element_type=fl)
    first_gain_grad = lax.optimization_barrier(jnp.sum(first_grad * normed1, axis=0))
    first_bias_grad = lax.optimization_barrier(jnp.sum(first_grad, axis=0))
    input_grad = resid_grad + norm_back(first_grad, normed1, scale1, first_gain)
    return (layer_out, input_grad, first_gain_grad, first_bias_grad, attention_in_grad, attention_out_grad, second_gain_grad, second_bias_grad, router_grad, expert_in_grad, expert_out_grad)
```

```python
import functools
import math

import jax
import jax.numpy as jnp
from jax import lax
from jax.experimental import pallas as pl
from jax.experimental.pallas import tpu as pltpu
from jax.sharding import PartitionSpec as P

HEAD_DIM = 64
SEQ = 197


EPS = 1e-06
GELU_C = math.sqrt(2.0 / math.pi)


def cut_along(shard, dim, devices):
    shape = shard.shape
    tiles = shard.reshape(*shape[:dim], devices, shape[dim] // devices, *shape[dim + 1 :])
    return jnp.moveaxis(tiles, dim, 0)


def sent_and_summed(shard, axis, dim):
    devices = lax.axis_size(axis)
    tiles = lax.all_to_all(cut_along(shard, dim, devices), axis, 0, 0, tiled=True)
    return jnp.sum(tiles.astype(jnp.float32), axis=0)


def sent_together(arrays, axis, dim, along):
    widths = [math.prod(a.shape[along:]) for a in arrays]
    both = jnp.concatenate(
        [a.reshape(*a.shape[:along], w) for a, w in zip(arrays, widths)], axis=along
    )
    out = sent_and_summed(both, axis, dim)
    tiles = jnp.split(out, [sum(widths[:k]) for k in range(1, len(widths))], axis=along)
    return tuple((b.reshape(*out.shape[:along], *a.shape[along:]) for a, b in zip(arrays, tiles)))


def normalize(values):
    centre = jnp.mean(values, axis=-1, keepdims=True)
    centred = values - centre
    spread = jnp.mean(centred * centred, axis=-1, keepdims=True)
    scale = lax.rsqrt(spread + EPS)
    return (centred * scale, scale)


def norm_back(grad_out, normed, scale, gain):
    scaled = grad_out * gain
    first_mean = jnp.mean(scaled, axis=-1, keepdims=True)
    second_mean = jnp.mean(scaled * normed, axis=-1, keepdims=True)
    return scale * (scaled - first_mean - normed * second_mean)


def gelu_parts(pre):
    inner = GELU_C * (pre + 0.044715 * pre * pre * pre)
    tangent = jnp.tanh(inner)
    value = 0.5 * pre * (1.0 + tangent)
    slope = 0.5 * (1.0 + tangent) + 0.5 * pre * (1.0 - tangent * tangent) * GELU_C * (
        1.0 + 3.0 * 0.044715 * pre * pre
    )
    return (value, slope)


MESH = pl.DeviceIdType.MESH


def greet(axes):
    barrier = pltpu.get_barrier_semaphore()
    peers = 0
    for axis in axes:
        devices = lax.axis_size(axis)
        me = lax.axis_index(axis)
        for k in range(1, devices):
            peer = lax.rem(me + k, devices)
            pl.semaphore_signal(barrier, inc=1, device_id={axis: peer}, device_id_type=MESH)
            peers += 1
    pl.semaphore_wait(barrier, peers)


def scatter_kernel(count, *refs):
    sources, targets = refs[:count], refs[count : 2 * count]
    send_sem, recv_sem = refs[2 * count :]
    devices = lax.axis_size("tensor")
    me = lax.axis_index("tensor")
    greet(("tensor",))
    copies = []
    for k in range(1, devices):
        peer = lax.rem(me + k, devices)
        for a in range(count):
            copy = pltpu.make_async_remote_copy(
                src_ref=sources[a].at[peer],
                dst_ref=targets[a].at[k],
                send_sem=send_sem.at[a, k],
                recv_sem=recv_sem.at[a, k],
                device_id={"tensor": peer},
                device_id_type=MESH,
            )
            copy.start()
            copies.append(copy)
    for a in range(count):
        targets[a][0] = sources[a][me]
    for copy in copies:
        copy.wait()


def scattered(arrays, collective_id):
    devices = lax.axis_size("tensor")
    count = len(arrays)
    return pl.pallas_call(
        functools.partial(scatter_kernel, count),
        out_shape=[jax.ShapeDtypeStruct(a.shape, a.dtype) for a in arrays],
        in_specs=[pl.BlockSpec(memory_space=pltpu.VMEM)] * count,
        out_specs=[pl.BlockSpec(memory_space=pltpu.VMEM)] * count,
        scratch_shapes=[
            pltpu.SemaphoreType.DMA((count, devices)),
            pltpu.SemaphoreType.DMA((count, devices)),
        ],
        compiler_params=pltpu.CompilerParams(collective_id=collective_id, has_side_effects=True),
        name=f"scatter{collective_id}",
    )(*arrays)


def gather_kernel(count, forward, *refs):
    sources, targets = refs[:count], refs[count : 2 * count]
    send_z, recv_z, send_x, recv_x = refs[2 * count :]
    devices = lax.axis_size("tensor")
    me = lax.axis_index("tensor")
    owners = lax.axis_size("expert") if forward else 1
    home = lax.axis_index("expert")
    greet(("tensor", "expert") if forward else ("tensor",))

    def across(a, k, source, place):
        copies = []
        for e in range(1, owners):
            copy = pltpu.make_async_remote_copy(
                src_ref=source,
                dst_ref=targets[a].at[e, place],
                send_sem=send_x.at[a, k, e],
                recv_sem=recv_x.at[a, k, e],
                device_id={"expert": lax.rem(home + e, owners)},
                device_id_type=MESH,
            )
            copy.start()
            copies.append(copy)
        return copies

    along = []
    for k in range(1, devices):
        peer = lax.rem(me + k, devices)
        for a in range(count):
            copy = pltpu.make_async_remote_copy(
                src_ref=sources[a],
                dst_ref=targets[a].at[0, me],
                send_sem=send_z.at[a, k],
                recv_sem=recv_z.at[a, k],
                device_id={"tensor": peer},
                device_id_type=MESH,
            )
            copy.start()
            along.append((a, k, copy))
    crossing = []
    for a in range(count):
        crossing += across(a, 0, sources[a], me)
    for a in range(count):
        targets[a][0, me] = sources[a][...]
    for a, k, copy in along:
        copy.wait()
        place = lax.rem(me + devices - k, devices)
        crossing += across(a, k, targets[a].at[0, place], place)
    for copy in crossing:
        copy.wait()


def gathered(arrays, collective_id, forward=False):
    devices = lax.axis_size("tensor")
    owners = lax.axis_size("expert") if forward else 1
    count = len(arrays)
    sems = [(count, devices)] * 2 + [(count, devices, owners)] * 2
    return pl.pallas_call(
        functools.partial(gather_kernel, count, forward),
        out_shape=[
            jax.ShapeDtypeStruct((owners, devices, *a.shape), a.dtype) for a in arrays
        ],
        in_specs=[pl.BlockSpec(memory_space=pltpu.VMEM)] * count,
        out_specs=[pl.BlockSpec(memory_space=pltpu.VMEM)] * count,
        scratch_shapes=[pltpu.SemaphoreType.DMA(s) for s in sems],
        compiler_params=pltpu.CompilerParams(collective_id=collective_id, has_side_effects=True),
        name=f"gather{collective_id}",
    )(*arrays)


def shifted(array, axis, offset):
    devices = lax.axis_size(axis)
    return lax.ppermute(array, axis, [(d, (d + offset) % devices) for d in range(devices)])


def from_owners(array):
    owners = lax.axis_size("expert")
    return jnp.stack([array] + [shifted(array, "expert", e) for e in range(1, owners)])


def to_owners(array):
    owners = lax.axis_size("expert")
    total = array[0].astype(jnp.float32)
    for e in range(1, owners):
        total = total + shifted(array[e], "expert", owners - e).astype(jnp.float32)
    return total


def rounded_up(value, multiple):
    return -(-value // multiple) * multiple


def per_device(
    inputs,
    first_gain,
    first_bias,
    attention_in,
    attention_out,
    second_gain,
    second_bias,
    router_weight,
    expert_in,
    expert_out,
    expert_ids,
    slot_index,
    cotangent,
):
    bf16, f32 = jnp.bfloat16, jnp.float32
    tokens_here = inputs.shape[0]
    model_width = inputs.shape[1]
    images = tokens_here // SEQ
    local_width = attention_in.shape[2]
    local_heads = local_width // HEAD_DIM
    owners = lax.axis_size("expert")
    cuts = lax.axis_size("tensor")
    experts_here = expert_in.shape[0]
    experts_all = experts_here * owners
    capacity = (2 * tokens_here - 1) // experts_all
    scaling = HEAD_DIM ** (-0.5)
    rows = rounded_up(rounded_up(tokens_here, cuts) // cuts, 8)
    padded = rows * cuts
    lanes = rounded_up(experts_all, 128)
    slots = rounded_up(owners * capacity, 16)
    piece = lax.axis_index("tensor")

    def split_heads(matrix):
        return matrix.reshape(images, SEQ, local_heads, HEAD_DIM)

    def pad_rows(matrix, value=0):
        return jnp.pad(
            matrix, ((0, padded - tokens_here), (0, 0)), constant_values=value
        )

    def my_rows(matrix):
        return lax.dynamic_slice_in_dim(pad_rows(matrix), piece * rows, rows, 0)

    target = jnp.where(slot_index < capacity, expert_ids * capacity + slot_index, -1)
    target_all = from_owners(pad_rows(target, -1).astype(f32).T)
    cot_all = from_owners(pad_rows(cotangent)).reshape(owners * padded, model_width)

    x_full = inputs.astype(f32)
    normed1, scale1 = normalize(x_full)
    first = (normed1 * first_gain + first_bias).astype(bf16)
    project = [
        jnp.dot(first, attention_in[which], preferred_element_type=f32).astype(bf16)
        for which in range(3)
    ]
    query_h, keys_h, values_h = [split_heads(part) for part in project]
    scores = jnp.einsum("iqhd,ikhd->ihqk", query_h, keys_h, preferred_element_type=f32) * scaling
    peak = jnp.max(scores, axis=-1, keepdims=True)
    logsum = peak[..., 0] + jnp.log(jnp.sum(jnp.exp(scores - peak), axis=-1))
    probs = jnp.exp(scores - logsum[..., None])
    weights = probs.astype(bf16)
    context_h = jnp.einsum(
        "ihqk,ikhd->iqhd", weights, values_h, preferred_element_type=f32
    ).astype(bf16)
    context = context_h.reshape(tokens_here, local_width)
    partial_attn = jnp.dot(pad_rows(context), attention_out, preferred_element_type=f32)
    (attn_parts,) = scattered([partial_attn.astype(bf16).reshape(cuts, rows, model_width)], 1)

    attended = jnp.sum(attn_parts.astype(f32), axis=0)
    resid = my_rows(inputs).astype(f32) + attended
    normed2, scale2 = normalize(resid)
    second = (normed2 * second_gain + second_bias).astype(bf16)
    logits = jnp.dot(second.astype(f32), router_weight, precision=lax.Precision.HIGHEST)
    route = jax.nn.softmax(logits, axis=-1)
    route_wide = jnp.pad(route, ((0, 0), (0, lanes - experts_all)))
    second_all, route_all = gathered([second, route_wide], 2, forward=True)
    second_all = second_all.reshape(owners * padded, model_width)
    route_all = route_all.reshape(owners * padded, lanes)

    base = lax.axis_index("expert") * experts_here
    block = jnp.arange(owners, dtype=jnp.int32)[:, None, None] * capacity
    place = target_all.astype(jnp.int32)
    local_row = jnp.arange(slots, dtype=jnp.int32)
    first_slot = (base + jnp.arange(experts_here, dtype=jnp.int32)) * capacity
    offset = place[None] - first_slot[:, None, None, None]
    row_of = jnp.where((offset >= 0) & (offset < capacity), offset + block[None], -1)
    picks = row_of[:, None] == local_row[None, :, None, None, None]
    chosen = jnp.any(picks, axis=3).reshape(experts_here, slots, owners * padded)
    placing = chosen.astype(bf16)
    route_here = lax.dynamic_slice_in_dim(route_all, base, experts_here, 1).T
    slot_gate = jnp.sum(jnp.where(chosen, route_here[:, None, :], 0.0), axis=-1)
    received = jnp.einsum("kct,td->kcd", placing, second_all, preferred_element_type=f32).astype(
        bf16
    )
    slotted = jnp.einsum("kct,td->kcd", placing, cot_all, preferred_element_type=f32)
    y_grad = (slot_gate[..., None] * slotted).astype(bf16)
    pre = jnp.einsum("kcd,kdf->kcf", received, expert_in, preferred_element_type=f32)
    value, slope = gelu_parts(pre)
    hidden = value.astype(bf16)
    partial_y = jnp.einsum("kcf,kfd->kcd", hidden, expert_out, preferred_element_type=f32)
    gated_y = (slot_gate[..., None] * partial_y).astype(bf16)
    mixed = jnp.einsum("kct,kcd->td", placing, gated_y, preferred_element_type=f32).astype(bf16)
    mixed_home = to_owners(mixed.reshape(owners, padded, model_width))
    slot_grad = jnp.sum(slotted * partial_y, axis=-1)
    route_part = jnp.sum(jnp.where(chosen, slot_grad[..., None], 0.0), axis=1)
    spot = jnp.arange(lanes, dtype=jnp.int32)[:, None] == base + jnp.arange(
        experts_here, dtype=jnp.int32
    )
    route_part = jnp.sum(
        jnp.where(spot[None], route_part.T[:, None, :], 0.0), axis=-1
    ).reshape(owners, padded, lanes)
    route_home = to_owners(route_part)
    hidden_grad = jnp.einsum("kcd,kfd->kcf", y_grad, expert_out, preferred_element_type=f32)
    pre_grad = (hidden_grad * slope).astype(bf16)
    partial_back = jnp.einsum("kcf,kdf->kcd", pre_grad, expert_in, preferred_element_type=f32)
    back = jnp.einsum(
        "kct,kcd->td", placing, partial_back.astype(bf16), preferred_element_type=f32
    ).astype(bf16)
    back_home = to_owners(back.reshape(owners, padded, model_width))
    local_out_grad = jnp.einsum("kcf,kcd->kfd", hidden, y_grad, preferred_element_type=f32)
    local_in_grad = jnp.einsum("kcd,kcf->kdf", received, pre_grad, preferred_element_type=f32)
    expert_in_grad, expert_out_grad = (
        lax.psum_scatter(
            local_in_grad.astype(bf16), "dp", scatter_dimension=1, tiled=True
        ).astype(f32),
        lax.psum_scatter(
            local_out_grad.astype(bf16), "dp", scatter_dimension=2, tiled=True
        ).astype(f32),
    )
    parts = scattered(
        [
            mixed_home.astype(bf16).reshape(cuts, rows, model_width),
            back_home.astype(bf16).reshape(cuts, rows, model_width),
            route_home.reshape(cuts, rows, lanes),
        ],
        3,
    )
    moe, back_rows, route_grad = [jnp.sum(part.astype(f32), axis=0) for part in parts]
    route_grad = route_grad[:, :experts_all]

    layer_rows = resid + moe
    grad_out = my_rows(cotangent).astype(f32)
    logit_grad = route * (route_grad - jnp.sum(route * route_grad, axis=-1, keepdims=True))
    local_router = jnp.dot(
        second.astype(f32).T, logit_grad, precision=lax.Precision.HIGHEST
    )
    second_grad = back_rows + jnp.dot(logit_grad, router_weight.T, precision=lax.Precision.HIGHEST)
    local_second_gain = jnp.sum(second_grad * normed2, axis=0)
    local_second_bias = jnp.sum(second_grad, axis=0)
    resid_grad = grad_out + norm_back(second_grad, normed2, scale2, second_gain)
    resid_all, layer_all = gathered([resid_grad.astype(bf16), layer_rows.astype(bf16)], 4)
    resid_low = resid_all.reshape(padded, model_width)[:tokens_here]
    layer_out = layer_all.reshape(padded, model_width)[:tokens_here].astype(f32)

    local_attn_out = jnp.einsum("rh,rd->hd", context, resid_low, preferred_element_type=f32)
    context_grad = jnp.einsum(
        "rd,hd->rh", resid_low, attention_out, preferred_element_type=f32
    ).astype(bf16)
    context_g = split_heads(context_grad)
    values_grad = jnp.einsum(
        "ihqk,iqhd->ikhd", weights, context_g, preferred_element_type=f32
    ).astype(bf16)
    probs_grad = jnp.einsum("iqhd,ikhd->ihqk", context_g, values_h, preferred_element_type=f32)
    delta = jnp.transpose(
        jnp.sum(context_g.astype(f32) * context_h.astype(f32), axis=-1), (0, 2, 1)
    )
    score_grad = (probs * (probs_grad - delta[..., None]) * scaling).astype(bf16)
    query_grad = jnp.einsum(
        "ihqk,ikhd->iqhd", score_grad, keys_h, preferred_element_type=f32
    ).astype(bf16)
    keys_grad = jnp.einsum(
        "ihqk,iqhd->ikhd", score_grad, query_h, preferred_element_type=f32
    ).astype(bf16)
    grads_flat = [
        part.reshape(tokens_here, local_width) for part in (query_grad, keys_grad, values_grad)
    ]
    partial_first = sum(
        jnp.einsum("rh,dh->rd", grads_flat[k], attention_in[k], preferred_element_type=f32)
        for k in range(3)
    )
    (first_parts,) = scattered(
        [pad_rows(partial_first).astype(bf16).reshape(cuts, rows, model_width)], 5
    )
    local_attn_in = jnp.stack(
        [
            jnp.einsum("rd,rh->dh", first, part, preferred_element_type=f32)
            for part in grads_flat
        ]
    )
    local_first_gain = jnp.sum(partial_first * normed1, axis=0)
    local_first_bias = jnp.sum(partial_first, axis=0)
    small = jnp.concatenate(
        [
            local_router.T,
            jnp.stack([local_first_gain, local_first_bias, local_second_gain, local_second_bias]),
        ]
    ).astype(bf16)
    small_sum = sent_and_summed(small, ("dp", "expert"), 1)
    attention_in_grad = sent_and_summed(local_attn_in.astype(bf16), ("dp", "expert"), 1)
    attention_out_grad = sent_and_summed(local_attn_out.astype(bf16), ("dp", "expert"), 1)

    first_grad = jnp.sum(first_parts.astype(f32), axis=0)
    normed1_rows, scale1_rows = normalize(my_rows(inputs).astype(f32))
    grad_rows = resid_grad + norm_back(first_grad, normed1_rows, scale1_rows, first_gain)
    tall = rounded_up(small_sum.shape[0], 8)
    wide = rounded_up(small_sum.shape[1], 128)
    small_pad = jnp.pad(
        small_sum, ((0, tall - small_sum.shape[0]), (0, wide - small_sum.shape[1]))
    )
    grad_all, small_all = gathered([grad_rows.astype(bf16), small_pad], 6)
    input_grad = grad_all.reshape(padded, model_width)[:tokens_here].astype(f32)
    totals = jnp.sum(small_all[0], axis=0)[: small_sum.shape[0], : small_sum.shape[1]]
    return (
        layer_out,
        input_grad,
        totals[experts_all],
        totals[experts_all + 1],
        attention_in_grad,
        attention_out_grad,
        totals[experts_all + 2],
        totals[experts_all + 3],
        totals[:experts_all].T,
        expert_in_grad,
        expert_out_grad,
    )


def solution(mesh):
    in_specs = (
        P(("dp", "expert"), None),
        P(),
        P(),
        P(None, None, "tensor"),
        P("tensor", None),
        P(),
        P(),
        P(),
        P("expert", None, "tensor"),
        P("expert", "tensor", None),
        P(("dp", "expert"), None),
        P(("dp", "expert"), None),
        P(("dp", "expert"), None),
    )
    out_specs = (
        P(("dp", "expert"), None),
        P(("dp", "expert"), None),
        P(("dp", "expert")),
        P(("dp", "expert")),
        P(None, ("dp", "expert"), "tensor"),
        P("tensor", ("dp", "expert")),
        P(("dp", "expert")),
        P(("dp", "expert")),
        P(("dp", "expert"), None),
        P("expert", "dp", "tensor"),
        P("expert", "tensor", "dp"),
    )
    return jax.shard_map(
        per_device, mesh=mesh, in_specs=in_specs, out_specs=out_specs, check_vma=False
    )
```

```python
import functools
import math

import jax
import jax.numpy as jnp
from jax import lax
from jax.experimental import pallas as pl
from jax.experimental.pallas import tpu as pltpu
from jax.sharding import PartitionSpec as P

HEAD_DIM = 64
SEQ = 197


EPS = 1e-06
GELU_C = math.sqrt(2.0 / math.pi)


def cut_along(shard, dim, devices):
    shape = shard.shape
    tiles = shard.reshape(*shape[:dim], devices, shape[dim] // devices, *shape[dim + 1 :])
    return jnp.moveaxis(tiles, dim, 0)


def sent_and_summed(shard, axis, dim):
    devices = lax.axis_size(axis)
    tiles = lax.all_to_all(cut_along(shard, dim, devices), axis, 0, 0, tiled=True)
    return jnp.sum(tiles.astype(jnp.float32), axis=0)


def sent_together(arrays, axis, dim, along):
    widths = [math.prod(a.shape[along:]) for a in arrays]
    both = jnp.concatenate(
        [a.reshape(*a.shape[:along], w) for a, w in zip(arrays, widths)], axis=along
    )
    out = sent_and_summed(both, axis, dim)
    tiles = jnp.split(out, [sum(widths[:k]) for k in range(1, len(widths))], axis=along)
    return tuple((b.reshape(*out.shape[:along], *a.shape[along:]) for a, b in zip(arrays, tiles)))


def normalize(values):
    centre = jnp.mean(values, axis=-1, keepdims=True)
    centred = values - centre
    spread = jnp.mean(centred * centred, axis=-1, keepdims=True)
    scale = lax.rsqrt(spread + EPS)
    return (centred * scale, scale)


def norm_back(grad_out, normed, scale, gain):
    scaled = grad_out * gain
    first_mean = jnp.mean(scaled, axis=-1, keepdims=True)
    second_mean = jnp.mean(scaled * normed, axis=-1, keepdims=True)
    return scale * (scaled - first_mean - normed * second_mean)


def gelu_parts(pre):
    inner = GELU_C * (pre + 0.044715 * pre * pre * pre)
    tangent = jnp.tanh(inner)
    value = 0.5 * pre * (1.0 + tangent)
    slope = 0.5 * (1.0 + tangent) + 0.5 * pre * (1.0 - tangent * tangent) * GELU_C * (
        1.0 + 3.0 * 0.044715 * pre * pre
    )
    return (value, slope)


MESH = pl.DeviceIdType.MESH


def greet(axes):
    barrier = pltpu.get_barrier_semaphore()
    peers = 0
    for axis in axes:
        devices = lax.axis_size(axis)
        me = lax.axis_index(axis)
        for k in range(1, devices):
            peer = lax.rem(me + k, devices)
            pl.semaphore_signal(barrier, inc=1, device_id={axis: peer}, device_id_type=MESH)
            peers += 1
    pl.semaphore_wait(barrier, peers)


def group_peer(k):
    owners = lax.axis_size("expert")
    members = lax.axis_size("dp") * owners
    me = lax.axis_index("dp") * owners + lax.axis_index("expert")
    peer = lax.rem(me + k, members)
    return {"dp": peer // owners, "expert": lax.rem(peer, owners)}


def greet_line_and_group(grouped):
    barrier = pltpu.get_barrier_semaphore()
    cuts = lax.axis_size("tensor")
    members = lax.axis_size("dp") * lax.axis_size("expert") if grouped else 1
    for k in range(1, cuts):
        peer = {"tensor": lax.rem(lax.axis_index("tensor") + k, cuts)}
        pl.semaphore_signal(barrier, inc=1, device_id=peer, device_id_type=MESH)
    for k in range(1, members):
        pl.semaphore_signal(barrier, inc=1, device_id=group_peer(k), device_id_type=MESH)
    pl.semaphore_wait(barrier, cuts + members - 2)


def group_copies(source, target, send_sem, recv_sem):
    owners = lax.axis_size("expert")
    members = lax.axis_size("dp") * owners
    me = lax.axis_index("dp") * owners + lax.axis_index("expert")
    copies = []
    for k in range(1, members):
        copy = pltpu.make_async_remote_copy(
            src_ref=source.at[lax.rem(me + k, members)],
            dst_ref=target.at[k],
            send_sem=send_sem.at[k],
            recv_sem=recv_sem.at[k],
            device_id=group_peer(k),
            device_id_type=MESH,
        )
        copy.start()
        copies.append(copy)
    target[0] = source[me]
    return copies


def ends_kernel(gather, *refs):
    source, group_source, target, group_target = refs[:4]
    send_sem, recv_sem, send_group, recv_group = refs[4:]
    devices = lax.axis_size("tensor")
    me = lax.axis_index("tensor")
    greet_line_and_group(True)
    copies = []
    for k in range(1, devices):
        peer = lax.rem(me + k, devices)
        copy = pltpu.make_async_remote_copy(
            src_ref=source if gather else source.at[peer],
            dst_ref=target.at[me] if gather else target.at[k],
            send_sem=send_sem.at[k],
            recv_sem=recv_sem.at[k],
            device_id={"tensor": peer},
            device_id_type=MESH,
        )
        copy.start()
        copies.append(copy)
    copies += group_copies(group_source, group_target, send_group, recv_group)
    if gather:
        target[me] = source[...]
    else:
        target[0] = source[me]
    for copy in copies:
        copy.wait()


def line_and_group(array, group_array, collective_id, gather):
    devices = lax.axis_size("tensor")
    members = group_array.shape[0]
    shape = (devices, *array.shape) if gather else array.shape
    return pl.pallas_call(
        functools.partial(ends_kernel, gather),
        out_shape=[
            jax.ShapeDtypeStruct(shape, array.dtype),
            jax.ShapeDtypeStruct(group_array.shape, group_array.dtype),
        ],
        in_specs=[pl.BlockSpec(memory_space=pltpu.VMEM)] * 2,
        out_specs=[pl.BlockSpec(memory_space=pltpu.VMEM)] * 2,
        scratch_shapes=[pltpu.SemaphoreType.DMA((n,)) for n in (devices, devices, members, members)],
        compiler_params=pltpu.CompilerParams(collective_id=collective_id, has_side_effects=True),
        name=f"ends{collective_id}",
    )(array, group_array)


def scatter_kernel(count, *refs):
    sources, targets = refs[:count], refs[count : 2 * count]
    send_sem, recv_sem = refs[2 * count :]
    devices = lax.axis_size("tensor")
    me = lax.axis_index("tensor")
    greet(("tensor",))
    copies = []
    for k in range(1, devices):
        peer = lax.rem(me + k, devices)
        for a in range(count):
            copy = pltpu.make_async_remote_copy(
                src_ref=sources[a].at[peer],
                dst_ref=targets[a].at[k],
                send_sem=send_sem.at[a, k],
                recv_sem=recv_sem.at[a, k],
                device_id={"tensor": peer},
                device_id_type=MESH,
            )
            copy.start()
            copies.append(copy)
    for a in range(count):
        targets[a][0] = sources[a][me]
    for copy in copies:
        copy.wait()


def scattered(arrays, collective_id):
    devices = lax.axis_size("tensor")
    count = len(arrays)
    return pl.pallas_call(
        functools.partial(scatter_kernel, count),
        out_shape=[jax.ShapeDtypeStruct(a.shape, a.dtype) for a in arrays],
        in_specs=[pl.BlockSpec(memory_space=pltpu.VMEM)] * count,
        out_specs=[pl.BlockSpec(memory_space=pltpu.VMEM)] * count,
        scratch_shapes=[
            pltpu.SemaphoreType.DMA((count, devices)),
            pltpu.SemaphoreType.DMA((count, devices)),
        ],
        compiler_params=pltpu.CompilerParams(collective_id=collective_id, has_side_effects=True),
        name=f"scatter{collective_id}",
    )(*arrays)


def gather_kernel(count, forward, *refs):
    sources, targets = refs[:count], refs[count : 2 * count]
    send_z, recv_z, send_x, recv_x = refs[2 * count :]
    devices = lax.axis_size("tensor")
    me = lax.axis_index("tensor")
    owners = lax.axis_size("expert") if forward else 1
    home = lax.axis_index("expert")
    greet(("tensor", "expert") if forward else ("tensor",))

    def across(a, k, source, place):
        copies = []
        for e in range(1, owners):
            copy = pltpu.make_async_remote_copy(
                src_ref=source,
                dst_ref=targets[a].at[e, place],
                send_sem=send_x.at[a, k, e],
                recv_sem=recv_x.at[a, k, e],
                device_id={"expert": lax.rem(home + e, owners)},
                device_id_type=MESH,
            )
            copy.start()
            copies.append(copy)
        return copies

    along = []
    for k in range(1, devices):
        peer = lax.rem(me + k, devices)
        for a in range(count):
            copy = pltpu.make_async_remote_copy(
                src_ref=sources[a],
                dst_ref=targets[a].at[0, me],
                send_sem=send_z.at[a, k],
                recv_sem=recv_z.at[a, k],
                device_id={"tensor": peer},
                device_id_type=MESH,
            )
            copy.start()
            along.append((a, k, copy))
    crossing = []
    for a in range(count):
        crossing += across(a, 0, sources[a], me)
    for a in range(count):
        targets[a][0, me] = sources[a][...]
    for a, k, copy in along:
        copy.wait()
        place = lax.rem(me + devices - k, devices)
        crossing += across(a, k, targets[a].at[0, place], place)
    for copy in crossing:
        copy.wait()


def gathered(arrays, collective_id, forward=False):
    devices = lax.axis_size("tensor")
    owners = lax.axis_size("expert") if forward else 1
    count = len(arrays)
    sems = [(count, devices)] * 2 + [(count, devices, owners)] * 2
    return pl.pallas_call(
        functools.partial(gather_kernel, count, forward),
        out_shape=[
            jax.ShapeDtypeStruct((owners, devices, *a.shape), a.dtype) for a in arrays
        ],
        in_specs=[pl.BlockSpec(memory_space=pltpu.VMEM)] * count,
        out_specs=[pl.BlockSpec(memory_space=pltpu.VMEM)] * count,
        scratch_shapes=[pltpu.SemaphoreType.DMA(s) for s in sems],
        compiler_params=pltpu.CompilerParams(collective_id=collective_id, has_side_effects=True),
        name=f"gather{collective_id}",
    )(*arrays)


def shifted(array, axis, offset):
    devices = lax.axis_size(axis)
    return lax.ppermute(array, axis, [(d, (d + offset) % devices) for d in range(devices)])


def from_owners(array):
    owners = lax.axis_size("expert")
    return jnp.stack([array] + [shifted(array, "expert", e) for e in range(1, owners)])


def to_owners(array):
    owners = lax.axis_size("expert")
    total = array[0].astype(jnp.float32)
    for e in range(1, owners):
        total = total + shifted(array[e], "expert", owners - e).astype(jnp.float32)
    return total


def rounded_up(value, multiple):
    return -(-value // multiple) * multiple


def experts_kernel(
    experts_all,
    slot_ref,
    spot_ref,
    second_ref,
    cot_ref,
    router_ref,
    in_ref,
    out_ref,
    mixed_ref,
    back_ref,
    share_ref,
    route_ref,
    cut_ref,
    placing_ref,
    gated_ref,
    low_ref,
    grad_ref,
):
    bf16, f32 = jnp.bfloat16, jnp.float32
    exact = lax.Precision.HIGHEST
    owners, padded, _ = second_ref.shape
    experts_here = in_ref.shape[0]
    lanes = router_ref.shape[1]
    depth = placing_ref.shape[2]

    def dot(a, b, a_dim, b_dim, precision=None):
        return lax.dot_general(
            a, b, (((a_dim,), (b_dim,)), ((), ())), precision=precision, preferred_element_type=f32
        )

    column = lax.broadcasted_iota(jnp.int32, (padded, lanes), 1)
    for o in range(owners):
        logits = dot(second_ref[o].astype(f32), router_ref[...], 1, 0, exact)
        logits = jnp.where(column < experts_all, logits, -1e30)
        lifted = jnp.exp(logits - jnp.max(logits, axis=-1, keepdims=True))
        lifted = jnp.where(column < experts_all, lifted, 0.0)
        route_ref[o] = lifted / jnp.sum(lifted, axis=-1, keepdims=True)
    slot = lax.broadcasted_iota(jnp.int32, (depth, padded), 0)
    for k in range(experts_here):
        gates, received, slotted = [], [], []
        for o in range(owners):
            picks = slot == slot_ref[k, o][None, :]
            placing = jnp.where(picks, 1.0, 0.0)
            low = placing.astype(bf16)
            placing_ref[k, o] = low
            chances = dot(placing, route_ref[o], 1, 0, exact)
            gates.append(jnp.sum(chances * spot_ref[k][None, :], axis=-1, keepdims=True))
            received.append(dot(low, second_ref[o], 1, 0).astype(bf16))
            slotted.append(dot(low, cot_ref[o], 1, 0))
        gate = jnp.concatenate(gates)
        received = jnp.concatenate(received)
        slotted = jnp.concatenate(slotted)
        y_grad = (gate * slotted).astype(bf16)
        value, slope = gelu_parts(dot(received, in_ref[k], 1, 0))
        hidden = value.astype(bf16)
        partial_y = dot(hidden, out_ref[k], 1, 0)
        gated_ref[k] = (gate * partial_y).astype(bf16)
        slot_grad = jnp.sum(slotted * partial_y, axis=-1, keepdims=True)
        grad_ref[k] = slot_grad * spot_ref[k][None, :]
        pre_grad = (dot(y_grad, out_ref[k], 1, 1) * slope).astype(bf16)
        low_ref[k] = dot(pre_grad, in_ref[k], 1, 1).astype(bf16)
        in_grad = dot(received, pre_grad, 0, 0).astype(bf16)
        out_grad = dot(y_grad, hidden, 0, 0).astype(bf16)
        blocks, _, _, share, _ = cut_ref.shape
        for d in range(blocks):
            cut_ref[d, 0, k] = in_grad[d * share : (d + 1) * share]
            cut_ref[d, 1, k] = out_grad[d * share : (d + 1) * share]
    for o in range(owners):
        span = pl.ds(o * depth, depth)
        here = range(experts_here)
        mixed_ref[o] = sum(
            dot(placing_ref[k, o], gated_ref[k, span], 0, 0) for k in here
        ).astype(bf16)
        back_ref[o] = sum(dot(placing_ref[k, o], low_ref[k, span], 0, 0) for k in here).astype(bf16)
        share_ref[o] = sum(
            dot(placing_ref[k, o].astype(f32), grad_ref[k, span], 0, 0, exact) for k in here
        )


def experts_block(slots, spot, second, cot, router, expert_in, expert_out, experts_all, depth):
    owners, padded, width = second.shape
    here, _, hidden = expert_in.shape
    lanes = router.shape[1]
    blocks = lax.axis_size("dp")
    bf16, f32 = jnp.bfloat16, jnp.float32
    shapes = [
        ((owners, padded, width), bf16),
        ((owners, padded, width), bf16),
        ((owners, padded, lanes), f32),
        ((owners, padded, lanes), f32),
        ((blocks, 2, here, width // blocks, hidden), bf16),
    ]
    return pl.pallas_call(
        functools.partial(experts_kernel, experts_all),
        out_shape=[jax.ShapeDtypeStruct(*s) for s in shapes],
        in_specs=[pl.BlockSpec(memory_space=pltpu.VMEM)] * 7,
        out_specs=[pl.BlockSpec(memory_space=pltpu.VMEM)] * 5,
        scratch_shapes=[
            pltpu.VMEM((here, owners, depth, padded), bf16),
            pltpu.VMEM((here, owners * depth, width), bf16),
            pltpu.VMEM((here, owners * depth, width), bf16),
            pltpu.VMEM((here, owners * depth, lanes), f32),
        ],
        compiler_params=pltpu.CompilerParams(
            vmem_limit_bytes=(32 << 20) if owners <= 2 else (60 << 20)
        ),
        name="experts",
    )(slots, spot, second, cot, router, expert_in, expert_out)


def per_device(
    inputs,
    first_gain,
    first_bias,
    attention_in,
    attention_out,
    second_gain,
    second_bias,
    router_weight,
    expert_in,
    expert_out,
    expert_ids,
    slot_index,
    cotangent,
):
    bf16, f32 = jnp.bfloat16, jnp.float32
    tokens_here = inputs.shape[0]
    model_width = inputs.shape[1]
    images = tokens_here // SEQ
    local_width = attention_in.shape[2]
    local_heads = local_width // HEAD_DIM
    owners = lax.axis_size("expert")
    cuts = lax.axis_size("tensor")
    experts_here = expert_in.shape[0]
    experts_all = experts_here * owners
    capacity = (2 * tokens_here - 1) // experts_all
    scaling = HEAD_DIM ** (-0.5)
    rows = rounded_up(rounded_up(tokens_here, cuts) // cuts, 8)
    padded = rows * cuts
    lanes = rounded_up(experts_all, 128)
    piece = lax.axis_index("tensor")

    def split_heads(matrix):
        return matrix.reshape(images, SEQ, local_heads, HEAD_DIM)

    def pad_rows(matrix, value=0):
        return jnp.pad(
            matrix, ((0, padded - tokens_here), (0, 0)), constant_values=value
        )

    def my_rows(matrix):
        return lax.dynamic_slice_in_dim(pad_rows(matrix), piece * rows, rows, 0)

    target = jnp.where(slot_index < capacity, expert_ids * capacity + slot_index, -1)
    target_all = from_owners(pad_rows(target, -1).astype(f32).T)
    cot_all = from_owners(pad_rows(cotangent))

    x_full = inputs.astype(f32)
    normed1, scale1 = normalize(x_full)
    first = (normed1 * first_gain + first_bias).astype(bf16)
    project = [
        jnp.dot(first, attention_in[which], preferred_element_type=f32).astype(bf16)
        for which in range(3)
    ]
    query_h, keys_h, values_h = [split_heads(part) for part in project]
    scores = jnp.einsum("iqhd,ikhd->ihqk", query_h, keys_h, preferred_element_type=f32) * scaling
    peak = jnp.max(scores, axis=-1, keepdims=True)
    logsum = peak[..., 0] + jnp.log(jnp.sum(jnp.exp(scores - peak), axis=-1))
    probs = jnp.exp(scores - logsum[..., None])
    weights = probs.astype(bf16)
    context_h = jnp.einsum(
        "ihqk,ikhd->iqhd", weights, values_h, preferred_element_type=f32
    ).astype(bf16)
    context = context_h.reshape(tokens_here, local_width)
    partial_attn = jnp.dot(pad_rows(context), attention_out, preferred_element_type=f32)
    (attn_parts,) = scattered([partial_attn.astype(bf16).reshape(cuts, rows, model_width)], 1)

    attended = jnp.sum(attn_parts.astype(f32), axis=0)
    resid = my_rows(inputs).astype(f32) + attended
    normed2, scale2 = normalize(resid)
    second = (normed2 * second_gain + second_bias).astype(bf16)
    (second_all,) = gathered([second], 2, forward=True)

    base = lax.axis_index("expert") * experts_here
    experts = base + jnp.arange(experts_here, dtype=jnp.int32)
    offset = target_all.astype(jnp.int32)[None] - (experts * capacity)[:, None, None, None]
    slots = jnp.max(jnp.where((offset >= 0) & (offset < capacity), offset, -1), axis=2)
    spot = (experts[:, None] == jnp.arange(lanes, dtype=jnp.int32)).astype(f32)
    mixed, back, share, route_all, expert_cuts = experts_block(
        slots,
        spot,
        second_all.reshape(owners, padded, model_width),
        cot_all,
        jnp.pad(router_weight, ((0, 0), (0, lanes - experts_all))),
        expert_in,
        expert_out,
        experts_all,
        rounded_up(capacity, 16),
    )
    route = lax.dynamic_slice_in_dim(route_all[0], piece * rows, rows, 0)[:, :experts_all]
    mixed_home = to_owners(mixed)
    back_home = to_owners(back)
    route_home = to_owners(share)
    expert_sums = jnp.sum(
        lax.all_to_all(expert_cuts, "dp", 0, 0, tiled=True).astype(f32), axis=0
    )
    expert_in_grad = expert_sums[0]
    expert_out_grad = jnp.swapaxes(expert_sums[1], 1, 2)
    parts = scattered(
        [
            mixed_home.astype(bf16).reshape(cuts, rows, model_width),
            back_home.astype(bf16).reshape(cuts, rows, model_width),
            route_home.reshape(cuts, rows, lanes),
        ],
        3,
    )
    moe, back_rows, route_grad = [jnp.sum(part.astype(f32), axis=0) for part in parts]
    route_grad = route_grad[:, :experts_all]

    layer_rows = resid + moe
    grad_out = my_rows(cotangent).astype(f32)
    logit_grad = route * (route_grad - jnp.sum(route * route_grad, axis=-1, keepdims=True))
    local_router = jnp.dot(
        second.astype(f32).T, logit_grad, precision=lax.Precision.HIGHEST
    )
    second_grad = back_rows + jnp.dot(logit_grad, router_weight.T, precision=lax.Precision.HIGHEST)
    local_second_gain = jnp.sum(second_grad * normed2, axis=0)
    local_second_bias = jnp.sum(second_grad, axis=0)
    resid_grad = grad_out + norm_back(second_grad, normed2, scale2, second_gain)
    resid_all, layer_all = gathered([resid_grad.astype(bf16), layer_rows.astype(bf16)], 4)
    resid_low = resid_all.reshape(padded, model_width)[:tokens_here]
    layer_out = layer_all.reshape(padded, model_width)[:tokens_here].astype(f32)

    context_grad = jnp.einsum(
        "rd,hd->rh", resid_low, attention_out, preferred_element_type=f32
    ).astype(bf16)
    context_g = split_heads(context_grad)
    values_grad = jnp.einsum(
        "ihqk,iqhd->ikhd", weights, context_g, preferred_element_type=f32
    ).astype(bf16)
    probs_grad = jnp.einsum("iqhd,ikhd->ihqk", context_g, values_h, preferred_element_type=f32)
    delta = jnp.transpose(
        jnp.sum(context_g.astype(f32) * context_h.astype(f32), axis=-1), (0, 2, 1)
    )
    score_grad = (probs * (probs_grad - delta[..., None]) * scaling).astype(bf16)
    query_grad = jnp.einsum(
        "ihqk,ikhd->iqhd", score_grad, keys_h, preferred_element_type=f32
    ).astype(bf16)
    keys_grad = jnp.einsum(
        "ihqk,iqhd->ikhd", score_grad, query_h, preferred_element_type=f32
    ).astype(bf16)
    grads_flat = [
        part.reshape(tokens_here, local_width) for part in (query_grad, keys_grad, values_grad)
    ]
    partial_first = sum(
        jnp.einsum("rh,dh->rd", grads_flat[k], attention_in[k], preferred_element_type=f32)
        for k in range(3)
    )
    local_first_gain = jnp.sum(partial_first * normed1, axis=0)
    local_first_bias = jnp.sum(partial_first, axis=0)
    members = lax.axis_size("dp") * owners
    share = model_width // members
    small = jnp.concatenate(
        [
            local_router.T,
            jnp.stack([local_first_gain, local_first_bias, local_second_gain, local_second_bias]),
        ]
    )
    tall = rounded_up(small.shape[0], 8)
    small = cut_along(small, 1, members)
    small = jnp.pad(
        small, ((0, 0), (0, tall - small.shape[1]), (0, rounded_up(share, 128) - share))
    )
    first_parts, small_parts = line_and_group(
        pad_rows(partial_first).astype(bf16).reshape(cuts, rows, model_width), small, 5, False
    )
    first_grad = jnp.sum(first_parts.astype(f32), axis=0)
    small_sum = jnp.sum(small_parts, axis=0)
    normed1_rows, scale1_rows = normalize(my_rows(inputs).astype(f32))
    grad_rows = resid_grad + norm_back(first_grad, normed1_rows, scale1_rows, first_gain)
    small_low = small_sum.astype(bf16)
    small_low = jnp.pad(small_low, ((0, rounded_up(tall, 16) - tall), (0, model_width - small_low.shape[1])))
    attention_cuts = jnp.stack(
        [
            jnp.einsum("rd,rh->dh", left, part, preferred_element_type=f32).astype(bf16)
            for left, part in zip([first] * 3 + [resid_low], grads_flat + [context])
        ],
        axis=1,
    ).reshape(members, share, 4, local_width)
    sent_rows = jnp.concatenate([grad_rows.astype(bf16), small_low])
    grad_all, attention_parts = line_and_group(
        sent_rows, jnp.swapaxes(attention_cuts, 1, 2), 6, True
    )
    input_grad = grad_all[:, :rows].reshape(padded, model_width)[:tokens_here].astype(f32)
    totals = jnp.sum(grad_all[:, rows:].astype(f32), axis=0)[:, :share]
    attention_sums = jnp.sum(attention_parts.astype(f32), axis=0)
    attention_in_grad = attention_sums[:3]
    attention_out_grad = attention_sums[3].T
    return (
        layer_out,
        input_grad,
        totals[experts_all],
        totals[experts_all + 1],
        attention_in_grad,
        attention_out_grad,
        totals[experts_all + 2],
        totals[experts_all + 3],
        totals[:experts_all].T,
        expert_in_grad,
        expert_out_grad,
    )


def solution(mesh):
    in_specs = (
        P(("dp", "expert"), None),
        P(),
        P(),
        P(None, None, "tensor"),
        P("tensor", None),
        P(),
        P(),
        P(),
        P("expert", None, "tensor"),
        P("expert", "tensor", None),
        P(("dp", "expert"), None),
        P(("dp", "expert"), None),
        P(("dp", "expert"), None),
    )
    out_specs = (
        P(("dp", "expert"), None),
        P(("dp", "expert"), None),
        P(("dp", "expert")),
        P(("dp", "expert")),
        P(None, ("dp", "expert"), "tensor"),
        P("tensor", ("dp", "expert")),
        P(("dp", "expert")),
        P(("dp", "expert")),
        P(("dp", "expert"), None),
        P("expert", "dp", "tensor"),
        P("expert", "tensor", "dp"),
    )
    return jax.shard_map(
        per_device, mesh=mesh, in_specs=in_specs, out_specs=out_specs, check_vma=False
    )
```

```python
import functools
import math

import jax
import jax.numpy as jnp
from jax import lax
from jax.experimental import pallas as pl
from jax.experimental.pallas import tpu as pltpu
from jax.sharding import PartitionSpec as P

HEAD_DIM = 64
SEQ = 197


EPS = 1e-06
GELU_C = math.sqrt(2.0 / math.pi)


def cut_along(shard, dim, devices):
    shape = shard.shape
    tiles = shard.reshape(*shape[:dim], devices, shape[dim] // devices, *shape[dim + 1 :])
    return jnp.moveaxis(tiles, dim, 0)


def sent_and_summed(shard, axis, dim):
    devices = lax.axis_size(axis)
    tiles = lax.all_to_all(cut_along(shard, dim, devices), axis, 0, 0, tiled=True)
    return jnp.sum(tiles.astype(jnp.float32), axis=0)


def sent_together(arrays, axis, dim, along):
    widths = [math.prod(a.shape[along:]) for a in arrays]
    both = jnp.concatenate(
        [a.reshape(*a.shape[:along], w) for a, w in zip(arrays, widths)], axis=along
    )
    out = sent_and_summed(both, axis, dim)
    tiles = jnp.split(out, [sum(widths[:k]) for k in range(1, len(widths))], axis=along)
    return tuple((b.reshape(*out.shape[:along], *a.shape[along:]) for a, b in zip(arrays, tiles)))


def normalize(values):
    centre = jnp.mean(values, axis=-1, keepdims=True)
    centred = values - centre
    spread = jnp.mean(centred * centred, axis=-1, keepdims=True)
    scale = lax.rsqrt(spread + EPS)
    return (centred * scale, scale)


def norm_back(grad_out, normed, scale, gain):
    scaled = grad_out * gain
    first_mean = jnp.mean(scaled, axis=-1, keepdims=True)
    second_mean = jnp.mean(scaled * normed, axis=-1, keepdims=True)
    return scale * (scaled - first_mean - normed * second_mean)


def gelu_parts(pre):
    inner = GELU_C * (pre + 0.044715 * pre * pre * pre)
    tangent = jnp.tanh(inner)
    value = 0.5 * pre * (1.0 + tangent)
    slope = 0.5 * (1.0 + tangent) + 0.5 * pre * (1.0 - tangent * tangent) * GELU_C * (
        1.0 + 3.0 * 0.044715 * pre * pre
    )
    return (value, slope)


MESH = pl.DeviceIdType.MESH


def greet(axes):
    barrier = pltpu.get_barrier_semaphore()
    peers = 0
    for axis in axes:
        devices = lax.axis_size(axis)
        me = lax.axis_index(axis)
        for k in range(1, devices):
            peer = lax.rem(me + k, devices)
            pl.semaphore_signal(barrier, inc=1, device_id={axis: peer}, device_id_type=MESH)
            peers += 1
    pl.semaphore_wait(barrier, peers)


def group_peer(k):
    owners = lax.axis_size("expert")
    members = lax.axis_size("dp") * owners
    me = lax.axis_index("dp") * owners + lax.axis_index("expert")
    peer = lax.rem(me + k, members)
    return {"dp": peer // owners, "expert": lax.rem(peer, owners)}


def greet_line_and_group(grouped):
    barrier = pltpu.get_barrier_semaphore()
    cuts = lax.axis_size("tensor")
    members = lax.axis_size("dp") * lax.axis_size("expert") if grouped else 1
    for k in range(1, cuts):
        peer = {"tensor": lax.rem(lax.axis_index("tensor") + k, cuts)}
        pl.semaphore_signal(barrier, inc=1, device_id=peer, device_id_type=MESH)
    for k in range(1, members):
        pl.semaphore_signal(barrier, inc=1, device_id=group_peer(k), device_id_type=MESH)
    pl.semaphore_wait(barrier, cuts + members - 2)


def group_copies(source, target, send_sem, recv_sem):
    owners = lax.axis_size("expert")
    members = lax.axis_size("dp") * owners
    me = lax.axis_index("dp") * owners + lax.axis_index("expert")
    copies = []
    for k in range(1, members):
        copy = pltpu.make_async_remote_copy(
            src_ref=source.at[lax.rem(me + k, members)],
            dst_ref=target.at[k],
            send_sem=send_sem.at[k],
            recv_sem=recv_sem.at[k],
            device_id=group_peer(k),
            device_id_type=MESH,
        )
        copy.start()
        copies.append(copy)
    target[0] = source[me]
    return copies


def ends_kernel(gather, *refs):
    source, group_source, target, group_target = refs[:4]
    send_sem, recv_sem, send_group, recv_group = refs[4:]
    devices = lax.axis_size("tensor")
    me = lax.axis_index("tensor")
    greet_line_and_group(True)
    copies = []
    for k in range(1, devices):
        peer = lax.rem(me + k, devices)
        copy = pltpu.make_async_remote_copy(
            src_ref=source if gather else source.at[peer],
            dst_ref=target.at[me] if gather else target.at[k],
            send_sem=send_sem.at[k],
            recv_sem=recv_sem.at[k],
            device_id={"tensor": peer},
            device_id_type=MESH,
        )
        copy.start()
        copies.append(copy)
    copies += group_copies(group_source, group_target, send_group, recv_group)
    if gather:
        target[me] = source[...]
    else:
        target[0] = source[me]
    for copy in copies:
        copy.wait()


def line_and_group(array, group_array, collective_id, gather):
    devices = lax.axis_size("tensor")
    members = group_array.shape[0]
    shape = (devices, *array.shape) if gather else array.shape
    return pl.pallas_call(
        functools.partial(ends_kernel, gather),
        out_shape=[
            jax.ShapeDtypeStruct(shape, array.dtype),
            jax.ShapeDtypeStruct(group_array.shape, group_array.dtype),
        ],
        in_specs=[pl.BlockSpec(memory_space=pltpu.VMEM)] * 2,
        out_specs=[pl.BlockSpec(memory_space=pltpu.VMEM)] * 2,
        scratch_shapes=[pltpu.SemaphoreType.DMA((n,)) for n in (devices, devices, members, members)],
        compiler_params=pltpu.CompilerParams(collective_id=collective_id, has_side_effects=True),
        name=f"ends{collective_id}",
    )(array, group_array)


def scatter_kernel(count, *refs):
    sources, targets = refs[:count], refs[count : 2 * count]
    send_sem, recv_sem = refs[2 * count :]
    devices = lax.axis_size("tensor")
    me = lax.axis_index("tensor")
    greet(("tensor",))
    copies = []
    for k in range(1, devices):
        peer = lax.rem(me + k, devices)
        for a in range(count):
            copy = pltpu.make_async_remote_copy(
                src_ref=sources[a].at[peer],
                dst_ref=targets[a].at[k],
                send_sem=send_sem.at[a, k],
                recv_sem=recv_sem.at[a, k],
                device_id={"tensor": peer},
                device_id_type=MESH,
            )
            copy.start()
            copies.append(copy)
    for a in range(count):
        targets[a][0] = sources[a][me]
    for copy in copies:
        copy.wait()


def scattered(arrays, collective_id):
    devices = lax.axis_size("tensor")
    count = len(arrays)
    return pl.pallas_call(
        functools.partial(scatter_kernel, count),
        out_shape=[jax.ShapeDtypeStruct(a.shape, a.dtype) for a in arrays],
        in_specs=[pl.BlockSpec(memory_space=pltpu.VMEM)] * count,
        out_specs=[pl.BlockSpec(memory_space=pltpu.VMEM)] * count,
        scratch_shapes=[
            pltpu.SemaphoreType.DMA((count, devices)),
            pltpu.SemaphoreType.DMA((count, devices)),
        ],
        compiler_params=pltpu.CompilerParams(collective_id=collective_id, has_side_effects=True),
        name=f"scatter{collective_id}",
    )(*arrays)


def gather_kernel(count, forward, *refs):
    sources, targets = refs[:count], refs[count : 2 * count]
    send_z, recv_z, send_x, recv_x = refs[2 * count :]
    devices = lax.axis_size("tensor")
    me = lax.axis_index("tensor")
    owners = lax.axis_size("expert") if forward else 1
    home = lax.axis_index("expert")
    greet(("tensor", "expert") if forward else ("tensor",))

    def across(a, k, source, place):
        copies = []
        for e in range(1, owners):
            copy = pltpu.make_async_remote_copy(
                src_ref=source,
                dst_ref=targets[a].at[e, place],
                send_sem=send_x.at[a, k, e],
                recv_sem=recv_x.at[a, k, e],
                device_id={"expert": lax.rem(home + e, owners)},
                device_id_type=MESH,
            )
            copy.start()
            copies.append(copy)
        return copies

    along = []
    for k in range(1, devices):
        peer = lax.rem(me + k, devices)
        for a in range(count):
            copy = pltpu.make_async_remote_copy(
                src_ref=sources[a],
                dst_ref=targets[a].at[0, me],
                send_sem=send_z.at[a, k],
                recv_sem=recv_z.at[a, k],
                device_id={"tensor": peer},
                device_id_type=MESH,
            )
            copy.start()
            along.append((a, k, copy))
    crossing = []
    for a in range(count):
        crossing += across(a, 0, sources[a], me)
    for a in range(count):
        targets[a][0, me] = sources[a][...]
    for a, k, copy in along:
        copy.wait()
        place = lax.rem(me + devices - k, devices)
        crossing += across(a, k, targets[a].at[0, place], place)
    for copy in crossing:
        copy.wait()


def gathered(arrays, collective_id, forward=False):
    devices = lax.axis_size("tensor")
    owners = lax.axis_size("expert") if forward else 1
    count = len(arrays)
    sems = [(count, devices)] * 2 + [(count, devices, owners)] * 2
    return pl.pallas_call(
        functools.partial(gather_kernel, count, forward),
        out_shape=[
            jax.ShapeDtypeStruct((owners, devices, *a.shape), a.dtype) for a in arrays
        ],
        in_specs=[pl.BlockSpec(memory_space=pltpu.VMEM)] * count,
        out_specs=[pl.BlockSpec(memory_space=pltpu.VMEM)] * count,
        scratch_shapes=[pltpu.SemaphoreType.DMA(s) for s in sems],
        compiler_params=pltpu.CompilerParams(collective_id=collective_id, has_side_effects=True),
        name=f"gather{collective_id}",
    )(*arrays)


def shifted(array, axis, offset):
    devices = lax.axis_size(axis)
    return lax.ppermute(array, axis, [(d, (d + offset) % devices) for d in range(devices)])


def from_owners(array):
    owners = lax.axis_size("expert")
    return jnp.stack([array] + [shifted(array, "expert", e) for e in range(1, owners)])


def to_owners(array):
    owners = lax.axis_size("expert")
    total = array[0].astype(jnp.float32)
    for e in range(1, owners):
        total = total + shifted(array[e], "expert", owners - e).astype(jnp.float32)
    return total


def rounded_up(value, multiple):
    return -(-value // multiple) * multiple


def experts_kernel(
    experts_all,
    slot_ref,
    spot_ref,
    second_ref,
    cot_ref,
    router_ref,
    in_ref,
    out_ref,
    mixed_ref,
    back_ref,
    share_ref,
    route_ref,
    cut_ref,
    placing_ref,
    gated_ref,
    low_ref,
    grad_ref,
):
    bf16, f32 = jnp.bfloat16, jnp.float32
    exact = lax.Precision.HIGHEST
    owners, padded, _ = second_ref.shape
    experts_here = in_ref.shape[0]
    lanes = router_ref.shape[1]
    depth = placing_ref.shape[2]

    def dot(a, b, a_dim, b_dim, precision=None):
        return lax.dot_general(
            a, b, (((a_dim,), (b_dim,)), ((), ())), precision=precision, preferred_element_type=f32
        )

    column = lax.broadcasted_iota(jnp.int32, (padded, lanes), 1)
    for o in range(owners):
        logits = dot(second_ref[o].astype(f32), router_ref[...], 1, 0, exact)
        logits = jnp.where(column < experts_all, logits, -1e30)
        lifted = jnp.exp(logits - jnp.max(logits, axis=-1, keepdims=True))
        lifted = jnp.where(column < experts_all, lifted, 0.0)
        route_ref[o] = lifted / jnp.sum(lifted, axis=-1, keepdims=True)
    slot = lax.broadcasted_iota(jnp.int32, (depth, padded), 0)
    for k in range(experts_here):
        gates, received, slotted = [], [], []
        for o in range(owners):
            picks = slot == slot_ref[k, o][None, :]
            placing = jnp.where(picks, 1.0, 0.0)
            low = placing.astype(bf16)
            placing_ref[k, o] = low
            chances = dot(placing, route_ref[o], 1, 0, exact)
            gates.append(jnp.sum(chances * spot_ref[k][None, :], axis=-1, keepdims=True))
            received.append(dot(low, second_ref[o], 1, 0).astype(bf16))
            slotted.append(dot(low, cot_ref[o], 1, 0))
        gate = jnp.concatenate(gates)
        received = jnp.concatenate(received)
        slotted = jnp.concatenate(slotted)
        y_grad = (gate * slotted).astype(bf16)
        value, slope = gelu_parts(dot(received, in_ref[k], 1, 0))
        hidden = value.astype(bf16)
        partial_y = dot(hidden, out_ref[k], 1, 0)
        gated_ref[k] = (gate * partial_y).astype(bf16)
        slot_grad = jnp.sum(slotted * partial_y, axis=-1, keepdims=True)
        grad_ref[k] = slot_grad * spot_ref[k][None, :]
        pre_grad = (dot(y_grad, out_ref[k], 1, 1) * slope).astype(bf16)
        low_ref[k] = dot(pre_grad, in_ref[k], 1, 1).astype(bf16)
        in_grad = dot(received, pre_grad, 0, 0).astype(bf16)
        out_grad = dot(y_grad, hidden, 0, 0).astype(bf16)
        blocks, _, _, share, _ = cut_ref.shape
        for d in range(blocks):
            cut_ref[d, 0, k] = in_grad[d * share : (d + 1) * share]
            cut_ref[d, 1, k] = out_grad[d * share : (d + 1) * share]
    for o in range(owners):
        span = pl.ds(o * depth, depth)
        here = range(experts_here)
        mixed_ref[o] = sum(
            dot(placing_ref[k, o], gated_ref[k, span], 0, 0) for k in here
        ).astype(bf16)
        back_ref[o] = sum(dot(placing_ref[k, o], low_ref[k, span], 0, 0) for k in here).astype(bf16)
        share_ref[o] = sum(
            dot(placing_ref[k, o].astype(f32), grad_ref[k, span], 0, 0, exact) for k in here
        )


def experts_block(slots, spot, second, cot, router, expert_in, expert_out, experts_all, depth):
    owners, padded, width = second.shape
    here, _, hidden = expert_in.shape
    lanes = router.shape[1]
    blocks = lax.axis_size("dp")
    bf16, f32 = jnp.bfloat16, jnp.float32
    shapes = [
        ((owners, padded, width), bf16),
        ((owners, padded, width), bf16),
        ((owners, padded, lanes), f32),
        ((owners, padded, lanes), f32),
        ((blocks, 2, here, width // blocks, hidden), bf16),
    ]
    return pl.pallas_call(
        functools.partial(experts_kernel, experts_all),
        out_shape=[jax.ShapeDtypeStruct(*s) for s in shapes],
        in_specs=[pl.BlockSpec(memory_space=pltpu.VMEM)] * 7,
        out_specs=[pl.BlockSpec(memory_space=pltpu.VMEM)] * 5,
        scratch_shapes=[
            pltpu.VMEM((here, owners, depth, padded), bf16),
            pltpu.VMEM((here, owners * depth, width), bf16),
            pltpu.VMEM((here, owners * depth, width), bf16),
            pltpu.VMEM((here, owners * depth, lanes), f32),
        ],
        compiler_params=pltpu.CompilerParams(
            vmem_limit_bytes=(32 << 20) if owners <= 2 else (60 << 20)
        ),
        name="experts",
    )(slots, spot, second, cot, router, expert_in, expert_out)


def per_device(
    inputs,
    first_gain,
    first_bias,
    attention_in,
    attention_out,
    second_gain,
    second_bias,
    router_weight,
    expert_in,
    expert_out,
    expert_ids,
    slot_index,
    cotangent,
):
    bf16, f32 = jnp.bfloat16, jnp.float32
    tokens_here = inputs.shape[0]
    model_width = inputs.shape[1]
    images = tokens_here // SEQ
    local_width = attention_in.shape[2]
    local_heads = local_width // HEAD_DIM
    owners = lax.axis_size("expert")
    cuts = lax.axis_size("tensor")
    experts_here = expert_in.shape[0]
    experts_all = experts_here * owners
    capacity = (2 * tokens_here - 1) // experts_all
    scaling = HEAD_DIM ** (-0.5)
    rows = rounded_up(rounded_up(tokens_here, cuts) // cuts, 8)
    padded = rows * cuts
    lanes = rounded_up(experts_all, 128)
    piece = lax.axis_index("tensor")

    def split_heads(matrix):
        return matrix.reshape(images, SEQ, local_heads, HEAD_DIM)

    def pad_rows(matrix, value=0):
        return jnp.pad(
            matrix, ((0, padded - tokens_here), (0, 0)), constant_values=value
        )

    def my_rows(matrix):
        return lax.dynamic_slice_in_dim(pad_rows(matrix), piece * rows, rows, 0)

    target = jnp.where(slot_index < capacity, expert_ids * capacity + slot_index, -1)
    target_all = from_owners(pad_rows(target, -1).astype(f32).T)
    cot_all = from_owners(pad_rows(cotangent))

    x_full = inputs.astype(f32)
    normed1, scale1 = normalize(x_full)
    first = (normed1 * first_gain + first_bias).astype(bf16)
    project = [
        jnp.dot(first, attention_in[which], preferred_element_type=f32).astype(bf16)
        for which in range(3)
    ]
    query_h, keys_h, values_h = [split_heads(part) for part in project]
    scores = jnp.einsum("iqhd,ikhd->ihqk", query_h, keys_h, preferred_element_type=f32) * scaling
    peak = jnp.max(scores, axis=-1, keepdims=True)
    logsum = peak[..., 0] + jnp.log(jnp.sum(jnp.exp(scores - peak), axis=-1))
    probs = jnp.exp(scores - logsum[..., None])
    weights = probs.astype(bf16)
    context_h = jnp.einsum(
        "ihqk,ikhd->iqhd", weights, values_h, preferred_element_type=f32
    ).astype(bf16)
    context = context_h.reshape(tokens_here, local_width)
    partial_attn = jnp.dot(pad_rows(context), attention_out, preferred_element_type=f32)
    (attn_parts,) = scattered([partial_attn.astype(bf16).reshape(cuts, rows, model_width)], 1)

    attended = jnp.sum(attn_parts.astype(f32), axis=0)
    resid = my_rows(inputs).astype(f32) + attended
    normed2, scale2 = normalize(resid)
    second = (normed2 * second_gain + second_bias).astype(bf16)
    (second_all,) = gathered([second], 2, forward=True)

    base = lax.axis_index("expert") * experts_here
    experts = base + jnp.arange(experts_here, dtype=jnp.int32)
    offset = target_all.astype(jnp.int32)[None] - (experts * capacity)[:, None, None, None]
    slots = jnp.max(jnp.where((offset >= 0) & (offset < capacity), offset, -1), axis=2)
    spot = (experts[:, None] == jnp.arange(lanes, dtype=jnp.int32)).astype(f32)
    mixed, back, share, route_all, expert_cuts = experts_block(
        slots,
        spot,
        second_all.reshape(owners, padded, model_width),
        cot_all,
        jnp.pad(router_weight, ((0, 0), (0, lanes - experts_all))),
        expert_in,
        expert_out,
        experts_all,
        rounded_up(capacity, 16),
    )
    route = lax.dynamic_slice_in_dim(route_all[0], piece * rows, rows, 0)[:, :experts_all]
    mixed_home = to_owners(mixed)
    back_home = to_owners(back)
    route_home = to_owners(share)
    expert_sums = jnp.sum(
        lax.all_to_all(expert_cuts, "dp", 0, 0, tiled=True).astype(f32), axis=0
    )
    expert_in_grad = expert_sums[0]
    expert_out_grad = jnp.swapaxes(expert_sums[1], 1, 2)
    parts = scattered(
        [
            mixed_home.astype(bf16).reshape(cuts, rows, model_width),
            back_home.astype(bf16).reshape(cuts, rows, model_width),
            route_home.reshape(cuts, rows, lanes),
        ],
        3,
    )
    moe, back_rows, route_grad = [jnp.sum(part.astype(f32), axis=0) for part in parts]
    route_grad = route_grad[:, :experts_all]

    layer_rows = resid + moe
    grad_out = my_rows(cotangent).astype(f32)
    logit_grad = route * (route_grad - jnp.sum(route * route_grad, axis=-1, keepdims=True))
    local_router = jnp.dot(
        second.astype(f32).T, logit_grad, precision=lax.Precision.HIGHEST
    )
    second_grad = back_rows + jnp.dot(logit_grad, router_weight.T, precision=lax.Precision.HIGHEST)
    local_second_gain = jnp.sum(second_grad * normed2, axis=0)
    local_second_bias = jnp.sum(second_grad, axis=0)
    resid_grad = grad_out + norm_back(second_grad, normed2, scale2, second_gain)
    (resid_all,) = gathered([resid_grad.astype(bf16)], 4)
    resid_low = resid_all.reshape(padded, model_width)[:tokens_here]

    context_grad = jnp.einsum(
        "rd,hd->rh", resid_low, attention_out, preferred_element_type=f32
    ).astype(bf16)
    context_g = split_heads(context_grad)
    values_grad = jnp.einsum(
        "ihqk,iqhd->ikhd", weights, context_g, preferred_element_type=f32
    ).astype(bf16)
    probs_grad = jnp.einsum("iqhd,ikhd->ihqk", context_g, values_h, preferred_element_type=f32)
    delta = jnp.transpose(
        jnp.sum(context_g.astype(f32) * context_h.astype(f32), axis=-1), (0, 2, 1)
    )
    score_grad = (probs * (probs_grad - delta[..., None]) * scaling).astype(bf16)
    query_grad = jnp.einsum(
        "ihqk,ikhd->iqhd", score_grad, keys_h, preferred_element_type=f32
    ).astype(bf16)
    keys_grad = jnp.einsum(
        "ihqk,iqhd->ikhd", score_grad, query_h, preferred_element_type=f32
    ).astype(bf16)
    grads_flat = [
        part.reshape(tokens_here, local_width) for part in (query_grad, keys_grad, values_grad)
    ]
    partial_first = sum(
        jnp.einsum("rh,dh->rd", grads_flat[k], attention_in[k], preferred_element_type=f32)
        for k in range(3)
    )
    local_first_gain = jnp.sum(partial_first * normed1, axis=0)
    local_first_bias = jnp.sum(partial_first, axis=0)
    members = lax.axis_size("dp") * owners
    share = model_width // members
    small = jnp.concatenate(
        [
            local_router.T,
            jnp.stack([local_first_gain, local_first_bias, local_second_gain, local_second_bias]),
        ]
    )
    tall = rounded_up(small.shape[0], 8)
    small = cut_along(small, 1, members)
    small = jnp.pad(
        small, ((0, 0), (0, tall - small.shape[1]), (0, rounded_up(share, 128) - share))
    )
    first_parts, small_parts = line_and_group(
        pad_rows(partial_first).astype(bf16).reshape(cuts, rows, model_width), small, 5, False
    )
    first_grad = jnp.sum(first_parts.astype(f32), axis=0)
    small_sum = jnp.sum(small_parts, axis=0)
    normed1_rows, scale1_rows = normalize(my_rows(inputs).astype(f32))
    grad_rows = resid_grad + norm_back(first_grad, normed1_rows, scale1_rows, first_gain)
    small_low = small_sum.astype(bf16)
    small_low = jnp.pad(small_low, ((0, rounded_up(tall, 16) - tall), (0, model_width - small_low.shape[1])))
    attention_cuts = jnp.stack(
        [
            jnp.einsum("rd,rh->dh", left, part, preferred_element_type=f32).astype(bf16)
            for left, part in zip([first] * 3 + [resid_low], grads_flat + [context])
        ],
        axis=1,
    ).reshape(members, share, 4, local_width)
    sent_rows = jnp.concatenate([grad_rows.astype(bf16), layer_rows.astype(bf16), small_low])
    grad_all, attention_parts = line_and_group(
        sent_rows, jnp.swapaxes(attention_cuts, 1, 2), 6, True
    )
    input_grad = grad_all[:, :rows].reshape(padded, model_width)[:tokens_here].astype(f32)
    layer_out = grad_all[:, rows : 2 * rows].reshape(padded, model_width)[:tokens_here].astype(f32)
    totals = jnp.sum(grad_all[:, 2 * rows :].astype(f32), axis=0)[:, :share]
    attention_sums = jnp.sum(attention_parts.astype(f32), axis=0)
    attention_in_grad = attention_sums[:3]
    attention_out_grad = attention_sums[3].T
    return (
        layer_out,
        input_grad,
        totals[experts_all],
        totals[experts_all + 1],
        attention_in_grad,
        attention_out_grad,
        totals[experts_all + 2],
        totals[experts_all + 3],
        totals[:experts_all].T,
        expert_in_grad,
        expert_out_grad,
    )


def solution(mesh):
    in_specs = (
        P(("dp", "expert"), None),
        P(),
        P(),
        P(None, None, "tensor"),
        P("tensor", None),
        P(),
        P(),
        P(),
        P("expert", None, "tensor"),
        P("expert", "tensor", None),
        P(("dp", "expert"), None),
        P(("dp", "expert"), None),
        P(("dp", "expert"), None),
    )
    out_specs = (
        P(("dp", "expert"), None),
        P(("dp", "expert"), None),
        P(("dp", "expert")),
        P(("dp", "expert")),
        P(None, ("dp", "expert"), "tensor"),
        P("tensor", ("dp", "expert")),
        P(("dp", "expert")),
        P(("dp", "expert")),
        P(("dp", "expert"), None),
        P("expert", "dp", "tensor"),
        P("expert", "tensor", "dp"),
    )
    return jax.shard_map(
        per_device, mesh=mesh, in_specs=in_specs, out_specs=out_specs, check_vma=False
    )
```
